512 devices in a mesh: op: 64 (over x, y, core), sec: 8 (over z).
Axes of the slice: x: 4, y: 8, z: 8, core: 2. Of those that a mesh axis runs over, the one named last changes fastest.
Arguments:
- wavefunction: bfloat16 [8, 512, 512], P('sec', 'op'), may hold values from -6 to 6
- left_ops: bfloat16 [2048, 512, 512], P(('op', 'sec')), may hold values from -0.25 to 0.25
- right_ops: bfloat16 [2048, 512, 512], P(('op', 'sec')), may hold values from -0.25 to 0.25
- in_sector: int32 [2048], P(('op', 'sec')), may hold values from 0 to 7
- counts: int32 [64, 8], replicated, may hold values from 1 to 4
Outputs:
- applied: bfloat16 [8, 512, 512], P('sec', 'op')
The draws below stay inside these ranges and needn't reach their ends.
Inputs may be any that keep to these rules, and one draw needn't show every extreme that they name: `counts`: a device's live terms are its first slots, as many as its count.
All inputs are finite; a program needn't handle non-finite values.
Results may differ from the reference program's by a relative error of at most 0.0049.
Values may be sent and summed in bfloat16 or wider, within the bound.
A program may use at most 64 MiB of HBM per device.

```python
import jax
import jax.numpy as jnp
from jax import lax

K = 512
RL = 512
SLOTS = 4
SECT = 8
TERMS = 2048
N_OP = 64
N_SEC = 8


def with_ends(drawn, own_key, smallest, largest):
    dims = drawn.shape
    place = [jax.random.randint(jax.random.fold_in(own_key, axis), (), 0, dims[axis]) for axis in range(len(dims))]
    drawn = drawn.at[tuple(place)].set(smallest)
    longest = dims.index(max(dims))
    place[longest] = (place[longest] + 1) % dims[longest]
    return drawn.at[tuple(place)].set(largest)


def levels(stream_key, dims, shards, smallest, top_value):
    level, own = 1.0, jax.random.fold_in(stream_key, 6)
    for position, parts in shards:
        steps = jnp.exp(jax.random.uniform(jax.random.fold_in(own, position), (parts,), jnp.float32, smallest / len(shards), top_value / len(shards)))
        level = level * jnp.repeat(steps, dims[position] // parts).reshape([-1 if axis == position else 1 for axis in range(len(dims))])
    return level


def scatter_about(rng, extent, scale, most, cuts=(), held_as=jnp.bfloat16):
    array = scale * jax.random.normal(rng, extent, jnp.float32)
    if cuts:
        array = array * levels(rng, extent, cuts, -0.22, 0.18)
    return jnp.clip(array, -most, most).astype(held_as)


def setup_inputs(seed: int = 0) -> dict:
    seeds = jax.random.split(jax.random.key(seed), 6)
    wavefunction = scatter_about(seeds[0], (SECT, K, K), 1.0, 6.0, ((0, 8), (1, 64)))
    left_ops = scatter_about(seeds[1], (TERMS, RL, K), K ** -0.5, 0.25, ((0, 512),))
    right_ops = scatter_about(seeds[2], (TERMS, K, K), K ** -0.5, 0.25, ((0, 512),))
    in_sector = with_ends(jax.random.randint(seeds[3], (TERMS,), 0, SECT), jax.random.fold_in(seeds[3], 1), 0, SECT - 1).astype(jnp.int32)
    counts = with_ends(jax.random.randint(seeds[4], (N_OP, N_SEC), 1, SLOTS + 1), jax.random.fold_in(seeds[4], 1), 1, SLOTS).astype(jnp.int32)
    return {"wavefunction": wavefunction, "left_ops": left_ops, "right_ops": right_ops, "in_sector": in_sector, "counts": counts}


def reference(wavefunction, left_ops, right_ops, in_sector, counts):
    positions = jnp.arange(TERMS, dtype=jnp.int32)
    device = positions // SLOTS
    slot_index = positions % SLOTS
    owner_op = device // N_SEC
    owner_sec = device % N_SEC
    living = slot_index < counts[owner_op, owner_sec]

    def accumulate(summed, pieces):
        left_block, right_block, sector, target, alive = pieces

        def add_term(current):
            sector_block = lax.dynamic_index_in_dim(wavefunction, sector, 0, keepdims=False)
            halfway = jnp.dot(left_block, sector_block, preferred_element_type=jnp.float32).astype(jnp.bfloat16)
            product = lax.dot_general(halfway, right_block, (((1,), (1,)), ((), ())), preferred_element_type=jnp.float32)
            previous = lax.dynamic_index_in_dim(current, target, 0, keepdims=False)
            return lax.dynamic_update_index_in_dim(current, previous + product, target, 0)

        def keep_sum(current):
            return current

        return lax.cond(alive, add_term, keep_sum, summed), None

    initial = jnp.zeros((SECT, RL, K), jnp.float32)
    summed, unused = lax.scan(accumulate, initial, (left_ops, right_ops, in_sector, owner_sec.astype(jnp.int32), living))
    factor = (N_OP * SLOTS) ** -0.5
    return (summed * factor).astype(jnp.bfloat16)
```

```python
import functools

import jax
import jax.numpy as jnp
from jax import lax
from jax.experimental import pallas as pl
from jax.experimental.pallas import tpu as pltpu
from jax.sharding import PartitionSpec as P

MESH = pl.DeviceIdType.MESH
NX, NY, NZ, NC = 4, 8, 8, 2
SIZES = {"x": NX, "y": NY, "z": NZ}
COLS = 128
UNITS = 4
CHUNKS = 2
ORDERS = (("z", "x", "y"), ("x", "y", "z"), ("z", "y", "x"), ("z", "x", "y"))


def kernel(
    wave_ref, left_ref, right_ref, sector_ref, counts_ref, out_ref,
    wbuf, lbuf, rbuf, pbuf, sibling_in, x_out, x_in, y_out, y_in,
    op_sem, own_sem, first_send, first_recv, second_send, second_recv,
    ring_send, ring_recv, twin_send, twin_recv,
    half_send, half_recv, x_send, x_recv, y_send, y_recv,
):
    op = lax.axis_index("op")
    z = lax.axis_index("sec")
    core = lax.rem(op, NC)
    y = lax.rem(lax.div(op, NC), NY)
    x = lax.div(op, NC * NY)
    me = {"x": x, "y": y, "z": z}
    twin = 1 - core
    slots = left_ref.shape[0]

    def device(place, which=None):
        which = core if which is None else which
        return {"op": (place["x"] * NY + place["y"]) * NC + which, "sec": place["z"]}

    def shifted(axis, by):
        n = SIZES[axis]
        return {**me, axis: lax.rem(me[axis] + (by % n), n)}

    def part(unit, place, which=None):
        which = core if which is None else which
        return wbuf.at[unit, place["z"], place["x"], place["y"], which]

    def send(src, dst, send_sem, recv_sem, to):
        pltpu.make_async_remote_copy(
            src_ref=src, dst_ref=dst, send_sem=send_sem, recv_sem=recv_sem,
            device_id=to, device_id_type=MESH,
        ).start()

    def take(ref, sem):
        pltpu.make_async_copy(ref, ref, sem).wait()

    loads = []
    for slot in range(slots):
        loads.append(pltpu.make_async_copy(left_ref.at[slot], lbuf.at[slot], op_sem.at[0, slot]))
        loads.append(pltpu.make_async_copy(right_ref.at[slot], rbuf.at[slot], op_sem.at[1, slot]))
    own = [
        pltpu.make_async_copy(wave_ref.at[0, :, pl.ds(COLS * unit, COLS)], part(unit, me), own_sem.at[unit])
        for unit in range(UNITS)
    ]
    for copy in own:
        copy.start()

    barrier = pltpu.get_barrier_semaphore()
    greeted = 1
    pl.semaphore_signal(barrier, inc=1, device_id=device(me, twin), device_id_type=MESH)
    for axis, n in SIZES.items():
        for by in range(1, n):
            pl.semaphore_signal(barrier, inc=1, device_id=device(shifted(axis, by)), device_id_type=MESH)
            greeted += 1
    for copy in loads:
        copy.start()
    pl.semaphore_wait(barrier, greeted)

    for unit, (first, _, _) in enumerate(ORDERS):
        for by in range(1, SIZES[first]):
            send(
                wave_ref.at[0, :, pl.ds(COLS * unit, COLS)], part(unit, me),
                first_send.at[unit], first_recv.at[unit], device(shifted(first, by)),
            )
    for unit, (first, second, _) in enumerate(ORDERS):
        rest = {**me, first: pl.ds(0, SIZES[first] - 1)}
        take(part(unit, rest), first_recv.at[unit])
        own[unit].wait()
        held = {**me, first: slice(None)}
        for by in range(1, SIZES[second]):
            send(
                part(unit, held), part(unit, held),
                second_send.at[unit], second_recv.at[unit], device(shifted(second, by)),
            )

    def slab(unit, origin, chunk, which=None):
        first, second, third = ORDERS[unit]
        length = SIZES[first] // CHUNKS
        return part(
            unit, {first: pl.ds(chunk * length, length), second: slice(None), third: origin}, which
        )

    def hand_over(unit, origin, chunk):
        piece = slab(unit, origin, chunk)
        send(piece, piece, twin_send.at[unit], twin_recv.at[unit], device(me, twin))

    def pieces(unit, step):
        half = SIZES[ORDERS[unit][2]] // 2
        if step > half:
            return ()
        if step == half:
            return tuple((chunk, 1 if chunk < CHUNKS // 2 else -1) for chunk in range(CHUNKS))
        return tuple((chunk, way) for chunk in range(CHUNKS) for way in (1, -1))

    def pass_on(unit, step, chunk, way):
        third = ORDERS[unit][2]
        origin = shifted(third, -way * (step - 1))[third]
        piece = slab(unit, origin, chunk)
        sem = ring_recv.at[unit, step - 1, chunk, (1 - way) // 2]
        send(piece, piece, ring_send.at[unit], sem, device(shifted(third, way)))

    for unit, (first, second, third) in enumerate(ORDERS):
        rest = {**me, first: slice(None), second: pl.ds(0, SIZES[second] - 1)}
        take(part(unit, rest), second_recv.at[unit])
        for chunk, way in pieces(unit, 1):
            pass_on(unit, 1, chunk, way)
        for chunk in range(CHUNKS):
            hand_over(unit, me[third], chunk)
    for step in range(1, max(SIZES.values()) // 2 + 1):
        for unit, (_, _, third) in enumerate(ORDERS):
            later = pieces(unit, step + 1)
            for chunk, way in pieces(unit, step):
                origin = shifted(third, -way * step)[third]
                take(slab(unit, origin, chunk), ring_recv.at[unit, step - 1, chunk, (1 - way) // 2])
                if (chunk, way) in later:
                    pass_on(unit, step + 1, chunk, way)
                hand_over(unit, origin, chunk)
    everything = {"x": slice(None), "y": slice(None), "z": slice(None)}
    for unit in range(UNITS):
        take(part(unit, everything, twin), twin_recv.at[unit])

    for copy in loads:
        copy.wait()
    alive_below = counts_ref[op, z]
    total = None
    for slot in range(slots):
        sector = sector_ref[slot]
        block = jnp.concatenate(
            [
                wbuf[unit, sector].astype(jnp.float32).reshape(-1, COLS).astype(jnp.bfloat16)
                for unit in range(UNITS)
            ],
            axis=1,
        )
        halfway = jnp.dot(lbuf[slot], block, preferred_element_type=jnp.float32)
        halfway = jnp.where(slot < alive_below, halfway, 0.0).astype(jnp.bfloat16)
        product = lax.dot_general(
            halfway, rbuf[slot], (((1,), (1,)), ((), ())), preferred_element_type=jnp.float32
        )
        total = product if total is None else total + product
    pbuf[...] = total.reshape(pbuf.shape)

    for by in range(NX):
        row = shifted("x", by)["x"]
        send(
            pbuf.at[row, :, twin], sibling_in.at[row], half_send, half_recv.at[by], device(me, twin)
        )
    kept = None
    for by in (*range(1, NX), 0):
        row = shifted("x", by)["x"]
        take(sibling_in.at[row], half_recv.at[by])
        both = pbuf[row, :, core] + sibling_in[row]
        if by:
            x_out[by - 1] = both.astype(jnp.bfloat16)
            send(
                x_out.at[by - 1], x_in.at[by - 1], x_send, x_recv.at[by - 1], device(shifted("x", by))
            )
        else:
            kept = both
    for by in range(1, NX):
        take(x_in.at[by - 1], x_recv.at[by - 1])
        kept = kept + x_in[by - 1].astype(jnp.float32)
    pbuf[x, :, core] = kept
    for by in range(1, NY):
        y_out[by - 1] = pbuf[x, shifted("y", by)["y"], core].astype(jnp.bfloat16)
        send(
            y_out.at[by - 1], y_in.at[by - 1], y_send, y_recv.at[by - 1], device(shifted("y", by))
        )
    result = pbuf[x, y, core]
    for by in range(1, NY):
        take(y_in.at[by - 1], y_recv.at[by - 1])
        result = result + y_in[by - 1].astype(jnp.float32)
    out_ref[0] = (result * (NX * NY * NC * slots) ** -0.5).astype(out_ref.dtype)

    for unit, (first, second, third) in enumerate(ORDERS):
        take(part(unit, {**me, first: pl.ds(0, SIZES[first] - 1)}), first_send.at[unit])
        take(
            part(unit, {**me, first: slice(None), second: pl.ds(0, SIZES[second] - 1)}),
            second_send.at[unit],
        )
        take(part(unit, {**everything, third: pl.ds(0, SIZES[third] - 1)}), ring_send.at[unit])
        take(part(unit, everything), twin_send.at[unit])
    take(sibling_in, half_send)
    take(x_out, x_send)
    take(y_out, y_send)


def shards(wavefunction, left_ops, right_ops, in_sector, counts):
    slots, rows, depth = left_ops.shape
    held = wavefunction.shape[1]
    columns = wavefunction.shape[2]
    dma = pltpu.SemaphoreType.DMA
    steps = max(SIZES.values()) // 2
    return pl.pallas_call(
        kernel,
        out_shape=jax.ShapeDtypeStruct(wavefunction.shape, wavefunction.dtype),
        in_specs=[
            pl.BlockSpec(memory_space=pltpu.VMEM),
            pl.BlockSpec(memory_space=pl.ANY),
            pl.BlockSpec(memory_space=pl.ANY),
            pl.BlockSpec(memory_space=pltpu.SMEM),
            pl.BlockSpec(memory_space=pltpu.SMEM),
        ],
        out_specs=pl.BlockSpec(memory_space=pltpu.VMEM),
        scratch_shapes=[
            pltpu.VMEM((UNITS, NZ, NX, NY, NC, held, COLS), jnp.bfloat16),
            pltpu.VMEM((slots, rows, depth), jnp.bfloat16),
            pltpu.VMEM((slots, columns, columns), jnp.bfloat16),
            pltpu.VMEM((NX, NY, NC, held, columns), jnp.float32),
            pltpu.VMEM((NX, NY, held, columns), jnp.float32),
            pltpu.VMEM((NX - 1, NY, held, columns), jnp.bfloat16),
            pltpu.VMEM((NX - 1, NY, held, columns), jnp.bfloat16),
            pltpu.VMEM((NY - 1, held, columns), jnp.bfloat16),
            pltpu.VMEM((NY - 1, held, columns), jnp.bfloat16),
            dma((2, slots)),
            dma((UNITS,)),
            dma((UNITS,)),
            dma((UNITS,)),
            dma((UNITS,)),
            dma((UNITS,)),
            dma((UNITS,)),
            dma((UNITS, steps, CHUNKS, 2)),
            dma((UNITS,)),
            dma((UNITS,)),
            dma,
            dma((NX,)),
            dma,
            dma((NX - 1,)),
            dma,
            dma((NY - 1,)),
        ],
        compiler_params=pltpu.CompilerParams(collective_id=0, has_side_effects=True),
    )(wavefunction, left_ops, right_ops, in_sector, counts)


def solution(mesh):
    placed = (
        P("sec", "op", None),
        P(("op", "sec"), None, None),
        P(("op", "sec"), None, None),
        P(("op", "sec")),
        P(),
    )
    return jax.shard_map(
        shards, mesh=mesh, in_specs=placed, out_specs=P("sec", "op", None), check_vma=False
    )
```

```python
import functools

import jax
import jax.numpy as jnp
from jax import lax
from jax.experimental import pallas as pl
from jax.experimental.pallas import tpu as pltpu
from jax.sharding import PartitionSpec as P

MESH = pl.DeviceIdType.MESH
NX, NY, NZ, NC = 4, 8, 8, 2
SIZES = {"x": NX, "y": NY, "z": NZ}
COLS = 256
LAST = ("y", "z")
UNITS = len(LAST)
SPREAD = {"y": "z", "z": "y"}
PEERS = NX * NY - 1
OFFSETS = [
    {"x": dx, "y": dy, "z": dz}
    for dx in range(NX)
    for dy in range(NY)
    for dz in range(NZ)
    if (dx or dy or dz) and not (dy and dz)
]


def kernel(
    wave_ref, left_ref, right_ref, sector_ref, counts_ref, out_ref,
    wbuf, lbuf, rbuf, pbuf, sibling_in, share_out, share_in,
    op_sem, own_sem, plane_send, plane_recv,
    ring_send, ring_recv, twin_send, twin_recv,
    half_send, half_recv, share_send, share_recv,
):
    op = lax.axis_index("op")
    z = lax.axis_index("sec")
    core = lax.rem(op, NC)
    y = lax.rem(lax.div(op, NC), NY)
    x = lax.div(op, NC * NY)
    me = {"x": x, "y": y, "z": z}
    twin = 1 - core
    slots = left_ref.shape[0]

    def device(place, which=None):
        which = core if which is None else which
        return {"op": (place["x"] * NY + place["y"]) * NC + which, "sec": place["z"]}

    def shifted(axis, by):
        n = SIZES[axis]
        return {**me, axis: lax.rem(me[axis] + (by % n), n)}

    def moved(offset):
        return {axis: lax.rem(me[axis] + offset[axis], SIZES[axis]) for axis in SIZES}

    def part(unit, place, which=None):
        which = core if which is None else which
        return wbuf.at[unit, place["z"], place["x"], place["y"], which]

    def send(src, dst, send_sem, recv_sem, to):
        pltpu.make_async_remote_copy(
            src_ref=src, dst_ref=dst, send_sem=send_sem, recv_sem=recv_sem,
            device_id=to, device_id_type=MESH,
        ).start()

    def take(ref, sem):
        pltpu.make_async_copy(ref, ref, sem).wait()

    loads = []
    for slot in range(slots):
        loads.append(pltpu.make_async_copy(left_ref.at[slot], lbuf.at[slot], op_sem.at[0, slot]))
        loads.append(pltpu.make_async_copy(right_ref.at[slot], rbuf.at[slot], op_sem.at[1, slot]))
    own = [
        pltpu.make_async_copy(wave_ref.at[0, :, pl.ds(COLS * unit, COLS)], part(unit, me), own_sem.at[unit])
        for unit in range(UNITS)
    ]
    for copy in own:
        copy.start()

    barrier = pltpu.get_barrier_semaphore()
    greeted = 1
    pl.semaphore_signal(barrier, inc=1, device_id=device(me, twin), device_id_type=MESH)
    for offset in OFFSETS:
        pl.semaphore_signal(barrier, inc=1, device_id=device(moved(offset)), device_id_type=MESH)
        greeted += 1
    for copy in loads:
        copy.start()
    for copy in own:
        copy.wait()
    pl.semaphore_wait(barrier, greeted)

    for unit, last in enumerate(LAST):
        for offset in OFFSETS:
            if not offset[last]:
                send(
                    part(unit, me), part(unit, me),
                    plane_send.at[unit], plane_recv.at[unit], device(moved(offset)),
                )

    def slab(unit, chunk, origin):
        last = LAST[unit]
        return part(unit, {"x": chunk, SPREAD[last]: slice(None), last: origin})

    def hand_over(unit, piece):
        send(piece, piece, twin_send.at[unit], twin_recv.at[unit], device(me, twin))

    def ways(chunk, step):
        if step < NY // 2:
            return (1, -1)
        return ((1, -1)[chunk % 2],) if step == NY // 2 else ()

    def ring_sem(unit, chunk, step, way):
        return ring_recv.at[unit, (step - 1) * NX + chunk, (1 - way) // 2]

    def pass_on(unit, chunk, step, way):
        last = LAST[unit]
        piece = slab(unit, chunk, shifted(last, -way * (step - 1))[last])
        send(
            piece, piece, ring_send.at[unit], ring_sem(unit, chunk, step, way),
            device(shifted(last, way)),
        )

    for unit, last in enumerate(LAST):
        take(share_in.at[:, :, pl.ds(0, COLS)], plane_recv.at[unit])
        for chunk in range(NX):
            for way in ways(chunk, 1):
                pass_on(unit, chunk, 1, way)
        for chunk in range(NX):
            hand_over(unit, slab(unit, chunk, me[last]))
    for step in range(1, NY // 2 + 1):
        for unit, last in enumerate(LAST):
            for chunk in range(NX):
                for way in ways(chunk, step):
                    piece = slab(unit, chunk, shifted(last, -way * step)[last])
                    take(piece, ring_sem(unit, chunk, step, way))
                    if way in ways(chunk, step + 1):
                        pass_on(unit, chunk, step + 1, way)
                    hand_over(unit, piece)
    everything = {"x": slice(None), "y": slice(None), "z": slice(None)}
    for unit in range(UNITS):
        take(part(unit, everything, twin), twin_recv.at[unit])

    for copy in loads:
        copy.wait()
    alive_below = counts_ref[z, op]
    total = None
    for slot in range(slots):
        sector = sector_ref[slot]
        block = jnp.concatenate(
            [
                wbuf[unit, sector].astype(jnp.float32).reshape(-1, COLS).astype(jnp.bfloat16)
                for unit in range(UNITS)
            ],
            axis=1,
        )
        halfway = jnp.dot(lbuf[slot], block, preferred_element_type=jnp.float32)
        halfway = jnp.where(slot < alive_below, halfway, 0.0).astype(jnp.bfloat16)
        product = lax.dot_general(
            halfway, rbuf[slot], (((1,), (1,)), ((), ())), preferred_element_type=jnp.float32
        )
        total = product if total is None else total + product
    pbuf[...] = total.reshape(pbuf.shape)

    for by in range(NX):
        row = shifted("x", by)["x"]
        send(
            pbuf.at[row, :, twin], sibling_in.at[row], half_send, half_recv.at[by], device(me, twin)
        )
    for by in (*range(1, NX), 0):
        row = shifted("x", by)["x"]
        take(sibling_in.at[row], half_recv.at[by])
        pbuf[row, :, core] = pbuf[row, :, core] + sibling_in[row]
        share_out[row] = pbuf[row, :, core].astype(jnp.bfloat16)
        for dy in range(NY):
            if by or dy:
                to = moved({"x": by, "y": dy, "z": 0})
                send(
                    share_out.at[to["x"], to["y"]], share_in.at[by * NY + dy - 1],
                    share_send, share_recv, device(to),
                )
    take(share_in, share_recv)
    result = pbuf[x, y, core] + jnp.sum(share_in[...].astype(jnp.float32), axis=0)
    out_ref[0] = (result * (NX * NY * NC * slots) ** -0.5).astype(out_ref.dtype)

    for unit, last in enumerate(LAST):
        take(share_in.at[:, :, pl.ds(0, COLS)], plane_send.at[unit])
        take(part(unit, {**everything, last: pl.ds(0, SIZES[last] - 1)}), ring_send.at[unit])
        take(part(unit, everything), twin_send.at[unit])
    take(sibling_in, half_send)
    take(share_in, share_send)


def shards(wavefunction, left_ops, right_ops, in_sector, counts):
    slots, rows, depth = left_ops.shape
    held = wavefunction.shape[1]
    columns = wavefunction.shape[2]
    dma = pltpu.SemaphoreType.DMA
    return pl.pallas_call(
        kernel,
        out_shape=jax.ShapeDtypeStruct(wavefunction.shape, wavefunction.dtype),
        in_specs=[
            pl.BlockSpec(memory_space=pltpu.VMEM),
            pl.BlockSpec(memory_space=pl.ANY),
            pl.BlockSpec(memory_space=pl.ANY),
            pl.BlockSpec(memory_space=pltpu.SMEM),
            pl.BlockSpec(memory_space=pltpu.SMEM),
        ],
        out_specs=pl.BlockSpec(memory_space=pltpu.VMEM),
        scratch_shapes=[
            pltpu.VMEM((UNITS, NZ, NX, NY, NC, held, COLS), jnp.bfloat16),
            pltpu.VMEM((slots, rows, depth), jnp.bfloat16),
            pltpu.VMEM((slots, columns, columns), jnp.bfloat16),
            pltpu.VMEM((NX, NY, NC, held, columns), jnp.float32),
            pltpu.VMEM((NX, NY, held, columns), jnp.float32),
            pltpu.VMEM((NX, NY, held, columns), jnp.bfloat16),
            pltpu.VMEM((PEERS, held, columns), jnp.bfloat16),
            dma((2, slots)),
            dma((UNITS,)),
            dma((UNITS,)),
            dma((UNITS,)),
            dma((UNITS,)),
            dma((UNITS, NX * NY // 2, 2)),
            dma((UNITS,)),
            dma((UNITS,)),
            dma,
            dma((NX,)),
            dma,
            dma,
        ],
        compiler_params=pltpu.CompilerParams(collective_id=0, has_side_effects=True),
    )(wavefunction, left_ops, right_ops, in_sector, counts.T)


def solution(mesh):
    placed = (
        P("sec", "op", None),
        P(("op", "sec"), None, None),
        P(("op", "sec"), None, None),
        P(("op", "sec")),
        P(),
    )
    return jax.shard_map(
        shards, mesh=mesh, in_specs=placed, out_specs=P("sec", "op", None), check_vma=False
    )
```

```python
import functools

import jax
import jax.numpy as jnp
from jax import lax
from jax.experimental import pallas as pl
from jax.experimental.pallas import tpu as pltpu
from jax.sharding import PartitionSpec as P

MESH = pl.DeviceIdType.MESH
NX, NY, NZ, NC = 4, 8, 8, 2
SIZES = {"x": NX, "y": NY, "z": NZ}
COLS = 256
LAST = ("y", "z")
UNITS = len(LAST)
SPREAD = {"y": "z", "z": "y"}
PEERS = NX * NY - 1


def hops(offset):
    return sum(min(by, SIZES[axis] - by) for axis, by in offset.items())


OFFSETS = sorted(
    (
        {"x": dx, "y": dy, "z": dz}
        for dx in range(NX)
        for dy in range(NY)
        for dz in range(NZ)
        if (dx or dy or dz) and not (dy and dz)
    ),
    key=lambda offset: -hops(offset),
)


def kernel(
    wave_ref, left_ref, right_ref, sector_ref, counts_ref, out_ref,
    wbuf, lbuf, rbuf, hbuf, pbuf, sibling_in, share_out, share_in,
    op_sem, own_sem, plane_send, plane_recv,
    ring_send, ring_recv, edge_recv, twin_send, twin_recv,
    half_send, half_recv, share_send, share_recv,
):
    op = lax.axis_index("op")
    z = lax.axis_index("sec")
    core = lax.rem(op, NC)
    y = lax.rem(lax.div(op, NC), NY)
    x = lax.div(op, NC * NY)
    me = {"x": x, "y": y, "z": z}
    twin = 1 - core
    slots = left_ref.shape[0]

    def device(place, which=None):
        which = core if which is None else which
        return {"op": (place["x"] * NY + place["y"]) * NC + which, "sec": place["z"]}

    def shifted(axis, by):
        n = SIZES[axis]
        return {**me, axis: lax.rem(me[axis] + (by % n), n)}

    def moved(offset):
        return {axis: lax.rem(me[axis] + offset[axis], SIZES[axis]) for axis in SIZES}

    def part(unit, place, which=None):
        which = core if which is None else which
        return wbuf.at[unit, place["z"], place["x"], place["y"], which]

    def send(src, dst, send_sem, recv_sem, to):
        pltpu.make_async_remote_copy(
            src_ref=src, dst_ref=dst, send_sem=send_sem, recv_sem=recv_sem,
            device_id=to, device_id_type=MESH,
        ).start()

    def take(ref, sem):
        pltpu.make_async_copy(ref, ref, sem).wait()

    loads = []
    for slot in range(slots):
        loads.append(pltpu.make_async_copy(left_ref.at[slot], lbuf.at[slot], op_sem.at[0, slot]))
        loads.append(pltpu.make_async_copy(right_ref.at[slot], rbuf.at[slot], op_sem.at[1, slot]))
    own = [
        pltpu.make_async_copy(wave_ref.at[0, :, pl.ds(COLS * unit, COLS)], part(unit, me), own_sem.at[unit])
        for unit in range(UNITS)
    ]
    for copy in own:
        copy.start()

    barrier = pltpu.get_barrier_semaphore()
    greeted = 1
    pl.semaphore_signal(barrier, inc=1, device_id=device(me, twin), device_id_type=MESH)
    for offset in OFFSETS:
        pl.semaphore_signal(barrier, inc=1, device_id=device(moved(offset)), device_id_type=MESH)
        greeted += 1
    for copy in loads:
        copy.start()
    for copy in own:
        copy.wait()
    pl.semaphore_wait(barrier, greeted)

    for unit, last in enumerate(LAST):
        for offset in OFFSETS:
            if not offset[last]:
                send(
                    part(unit, me), part(unit, me),
                    plane_send.at[unit], plane_recv.at[unit], device(moved(offset)),
                )

    def slab(unit, chunk, origin):
        last = LAST[unit]
        return part(unit, {"x": chunk, SPREAD[last]: slice(None), last: origin})

    def hand_over(unit, piece):
        send(piece, piece, twin_send.at[unit], twin_recv.at[unit], device(me, twin))

    def ways(chunk, step):
        if step < NY // 2:
            return (1, -1)
        return ((1, -1)[chunk % 2],) if step == NY // 2 else ()

    def ring_sem(unit, chunk, step, way):
        return ring_recv.at[unit, (step - 1) * NX + chunk, (1 - way) // 2]

    def pass_on(unit, chunk, step, way):
        last = LAST[unit]
        piece = slab(unit, chunk, shifted(last, -way * (step - 1))[last])
        send(
            piece, piece, ring_send.at[unit], ring_sem(unit, chunk, step, way),
            device(shifted(last, way)),
        )
        if step == NY // 2:
            send(
                piece, piece, ring_send.at[unit], edge_recv.at[unit], device(shifted(last, way), twin)
            )

    for unit, last in enumerate(LAST):
        take(share_in.at[:, :, pl.ds(0, COLS)], plane_recv.at[unit])
        for chunk in range(NX):
            for way in ways(chunk, 1):
                pass_on(unit, chunk, 1, way)
        for chunk in range(NX):
            hand_over(unit, slab(unit, chunk, me[last]))
    for step in range(1, NY // 2 + 1):
        for chunk in range(NX):
            for unit, last in enumerate(LAST):
                for way in ways(chunk, step):
                    piece = slab(unit, chunk, shifted(last, -way * step)[last])
                    take(piece, ring_sem(unit, chunk, step, way))
                    if way in ways(chunk, step + 1):
                        pass_on(unit, chunk, step + 1, way)
                    if step < NY // 2:
                        hand_over(unit, piece)
    everything = {"x": slice(None), "y": slice(None), "z": slice(None)}
    for unit in range(UNITS):
        most = {**everything, LAST[unit]: pl.ds(0, SIZES[LAST[unit]] - 1)}
        take(part(unit, most, twin), twin_recv.at[unit])
        take(part(unit, {**everything, LAST[unit]: 0}, twin), edge_recv.at[unit])

    for copy in loads:
        copy.wait()
    alive_below = counts_ref[z, op]
    for slot in range(slots):
        sector = sector_ref[slot]
        block = jnp.concatenate(
            [
                wbuf[unit, sector].astype(jnp.float32).reshape(-1, COLS).astype(jnp.bfloat16)
                for unit in range(UNITS)
            ],
            axis=1,
        )
        halfway = jnp.dot(lbuf[slot], block, preferred_element_type=jnp.float32)
        hbuf[slot] = jnp.where(slot < alive_below, halfway, 0.0).astype(jnp.bfloat16)

    length = hbuf.shape[1] // NX
    for pair in ((2, 1), (3, 0)):
        rows = [shifted("x", by)["x"] for by in pair]
        total = None
        for slot in range(slots):
            halfway = jnp.concatenate(
                [hbuf[slot, pl.ds(pl.multiple_of(row * length, length), length)] for row in rows]
            )
            product = lax.dot_general(
                halfway, rbuf[slot], (((1,), (1,)), ((), ())), preferred_element_type=jnp.float32
            )
            total = product if total is None else total + product
        total = total.reshape(len(pair), *pbuf.shape[1:])
        for place, (by, row) in enumerate(zip(pair, rows)):
            pbuf[row] = total[place]
            send(
                pbuf.at[row, :, twin], sibling_in.at[row], half_send, half_recv.at[by],
                device(me, twin),
            )
    for by in (2, 1, 3, 0):
        row = shifted("x", by)["x"]
        take(sibling_in.at[row], half_recv.at[by])
        pbuf[row, :, core] = pbuf[row, :, core] + sibling_in[row]
        share_out[row] = pbuf[row, :, core].astype(jnp.bfloat16)
        for dy in (4, 3, 5, 2, 6, 1, 7, 0):
            if by or dy:
                to = moved({"x": by, "y": dy, "z": 0})
                send(
                    share_out.at[to["x"], to["y"]], share_in.at[by * NY + dy - 1],
                    share_send, share_recv, device(to),
                )
    take(share_in, share_recv)
    result = pbuf[x, y, core] + jnp.sum(share_in[...].astype(jnp.float32), axis=0)
    out_ref[0] = (result * (NX * NY * NC * slots) ** -0.5).astype(out_ref.dtype)

    for unit, last in enumerate(LAST):
        take(share_in.at[:, :, pl.ds(0, COLS)], plane_send.at[unit])
        take(part(unit, everything), ring_send.at[unit])
        take(part(unit, {**everything, last: pl.ds(0, SIZES[last] - 1)}), twin_send.at[unit])
    take(sibling_in, half_send)
    take(share_in, share_send)


def shards(wavefunction, left_ops, right_ops, in_sector, counts):
    slots, rows, depth = left_ops.shape
    held = wavefunction.shape[1]
    columns = wavefunction.shape[2]
    dma = pltpu.SemaphoreType.DMA
    return pl.pallas_call(
        kernel,
        out_shape=jax.ShapeDtypeStruct(wavefunction.shape, wavefunction.dtype),
        in_specs=[
            pl.BlockSpec(memory_space=pltpu.VMEM),
            pl.BlockSpec(memory_space=pl.ANY),
            pl.BlockSpec(memory_space=pl.ANY),
            pl.BlockSpec(memory_space=pltpu.SMEM),
            pl.BlockSpec(memory_space=pltpu.SMEM),
        ],
        out_specs=pl.BlockSpec(memory_space=pltpu.VMEM),
        scratch_shapes=[
            pltpu.VMEM((UNITS, NZ, NX, NY, NC, held, COLS), jnp.bfloat16),
            pltpu.VMEM((slots, rows, depth), jnp.bfloat16),
            pltpu.VMEM((slots, columns, columns), jnp.bfloat16),
            pltpu.VMEM((slots, rows, columns), jnp.bfloat16),
            pltpu.VMEM((NX, NY, NC, held, columns), jnp.float32),
            pltpu.VMEM((NX, NY, held, columns), jnp.float32),
            pltpu.VMEM((NX, NY, held, columns), jnp.bfloat16),
            pltpu.VMEM((PEERS, held, columns), jnp.bfloat16),
            dma((2, slots)),
            dma((UNITS,)),
            dma((UNITS,)),
            dma((UNITS,)),
            dma((UNITS,)),
            dma((UNITS, NX * NY // 2, 2)),
            dma((UNITS,)),
            dma((UNITS,)),
            dma((UNITS,)),
            dma,
            dma((NX,)),
            dma,
            dma,
        ],
        compiler_params=pltpu.CompilerParams(collective_id=0, has_side_effects=True),
    )(wavefunction, left_ops, right_ops, in_sector, counts.T)


def solution(mesh):
    placed = (
        P("sec", "op", None),
        P(("op", "sec"), None, None),
        P(("op", "sec"), None, None),
        P(("op", "sec")),
        P(),
    )
    return jax.shard_map(
        shards, mesh=mesh, in_specs=placed, out_specs=P("sec", "op", None), check_vma=False
    )
```

```python
import functools

import jax
import jax.numpy as jnp
from jax import lax
from jax.experimental import pallas as pl
from jax.experimental.pallas import tpu as pltpu
from jax.sharding import PartitionSpec as P

MESH = pl.DeviceIdType.MESH
NX, NY, NZ, NC = 4, 8, 8, 2
SIZES = {"x": NX, "y": NY, "z": NZ}
COLS = 256
LAST = ("y", "z")
UNITS = len(LAST)
SPREAD = {"y": "z", "z": "y"}
PEERS = NX * NY - 1


def hops(offset):
    return sum(min(by, SIZES[axis] - by) for axis, by in offset.items())


OFFSETS = sorted(
    (
        {"x": dx, "y": dy, "z": dz}
        for dx in range(NX)
        for dy in range(NY)
        for dz in range(NZ)
        if (dx or dy or dz) and not (dy and dz)
    ),
    key=lambda offset: -hops(offset),
)


def kernel(
    wave_ref, left_ref, right_ref, sector_ref, counts_ref, out_ref,
    wbuf, lbuf, rbuf, hbuf, pbuf, sibling_in, share_out, share_in,
    op_sem, own_sem, plane_send, plane_recv,
    ring_send, ring_recv, edge_recv, twin_send, twin_recv,
    half_send, half_recv, share_send, share_recv,
):
    op = lax.axis_index("op")
    z = lax.axis_index("sec")
    core = lax.rem(op, NC)
    y = lax.rem(lax.div(op, NC), NY)
    x = lax.div(op, NC * NY)
    me = {"x": x, "y": y, "z": z}
    twin = 1 - core
    slots = left_ref.shape[0]

    def device(place, which=None):
        which = core if which is None else which
        return {"op": (place["x"] * NY + place["y"]) * NC + which, "sec": place["z"]}

    def shifted(axis, by):
        n = SIZES[axis]
        return {**me, axis: lax.rem(me[axis] + (by % n), n)}

    def moved(offset):
        return {axis: lax.rem(me[axis] + offset[axis], SIZES[axis]) for axis in SIZES}

    def part(unit, place, which=None):
        which = core if which is None else which
        return wbuf.at[unit, place["z"], place["x"], place["y"], which]

    def send(src, dst, send_sem, recv_sem, to):
        pltpu.make_async_remote_copy(
            src_ref=src, dst_ref=dst, send_sem=send_sem, recv_sem=recv_sem,
            device_id=to, device_id_type=MESH,
        ).start()

    def take(ref, sem):
        pltpu.make_async_copy(ref, ref, sem).wait()

    loads = []
    for slot in range(slots):
        loads.append(pltpu.make_async_copy(left_ref.at[slot], lbuf.at[slot], op_sem.at[0, slot]))
        loads.append(pltpu.make_async_copy(right_ref.at[slot], rbuf.at[slot], op_sem.at[1, slot]))
    own = [
        pltpu.make_async_copy(wave_ref.at[0, :, pl.ds(COLS * unit, COLS)], part(unit, me), own_sem.at[unit])
        for unit in range(UNITS)
    ]
    for copy in own:
        copy.start()

    barrier = pltpu.get_barrier_semaphore()
    greeted = 1
    pl.semaphore_signal(barrier, inc=1, device_id=device(me, twin), device_id_type=MESH)
    for offset in OFFSETS:
        pl.semaphore_signal(barrier, inc=1, device_id=device(moved(offset)), device_id_type=MESH)
        greeted += 1
    for copy in own:
        copy.wait()
    pl.semaphore_wait(barrier, greeted)

    for offset in OFFSETS:
        for unit, last in enumerate(LAST):
            if not offset[last]:
                send(
                    part(unit, me), part(unit, me),
                    plane_send.at[unit], plane_recv.at[unit], device(moved(offset)),
                )

    for copy in loads:
        copy.start()

    def slab(unit, chunk, origin):
        last = LAST[unit]
        return part(unit, {"x": chunk, SPREAD[last]: slice(None), last: origin})

    def hand_over(unit, piece):
        send(piece, piece, twin_send.at[unit], twin_recv.at[unit], device(me, twin))

    def ways(chunk, step):
        if step < NY // 2:
            return (1, -1)
        return ((1, -1)[chunk % 2],) if step == NY // 2 else ()

    def ring_sem(unit, chunk, step, way):
        return ring_recv.at[unit, (step - 1) * NX + chunk, (1 - way) // 2]

    def pass_on(unit, chunk, step, way):
        last = LAST[unit]
        piece = slab(unit, chunk, shifted(last, -way * (step - 1))[last])
        send(
            piece, piece, ring_send.at[unit], ring_sem(unit, chunk, step, way),
            device(shifted(last, way)),
        )
        if step == NY // 2:
            send(
                piece, piece, ring_send.at[unit], edge_recv.at[unit], device(shifted(last, way), twin)
            )

    for unit, last in enumerate(LAST):
        take(share_in.at[:, :, pl.ds(0, COLS)], plane_recv.at[unit])
        for chunk in range(NX):
            for way in ways(chunk, 1):
                pass_on(unit, chunk, 1, way)
        for chunk in range(NX):
            hand_over(unit, slab(unit, chunk, me[last]))
    for step in range(1, NY // 2 + 1):
        for chunk in range(NX):
            for unit, last in enumerate(LAST):
                for way in ways(chunk, step):
                    piece = slab(unit, chunk, shifted(last, -way * step)[last])
                    take(piece, ring_sem(unit, chunk, step, way))
                    if way in ways(chunk, step + 1):
                        pass_on(unit, chunk, step + 1, way)
                    if step < NY // 2:
                        hand_over(unit, piece)
    everything = {"x": slice(None), "y": slice(None), "z": slice(None)}
    for unit in range(UNITS):
        most = {**everything, LAST[unit]: pl.ds(0, SIZES[LAST[unit]] - 1)}
        take(part(unit, most, twin), twin_recv.at[unit])
        take(part(unit, {**everything, LAST[unit]: 0}, twin), edge_recv.at[unit])

    for copy in loads:
        copy.wait()
    alive_below = counts_ref[z, op]
    for slot in range(slots):
        sector = sector_ref[slot]
        block = jnp.concatenate(
            [
                wbuf[unit, sector].reshape(-1, COLS)
                for unit in range(UNITS)
            ],
            axis=1,
        )
        halfway = jnp.dot(lbuf[slot], block, preferred_element_type=jnp.float32)
        hbuf[slot] = jnp.where(slot < alive_below, halfway, 0.0).astype(jnp.bfloat16)

    length = hbuf.shape[1] // NX
    for pair in ((2, 1), (3, 0)):
        rows = [shifted("x", by)["x"] for by in pair]
        total = None
        for slot in range(slots):
            halfway = jnp.concatenate(
                [hbuf[slot, pl.ds(pl.multiple_of(row * length, length), length)] for row in rows]
            )
            product = lax.dot_general(
                halfway, rbuf[slot], (((1,), (1,)), ((), ())), preferred_element_type=jnp.float32
            )
            total = product if total is None else total + product
        total = total.reshape(len(pair), *pbuf.shape[1:])
        for place, (by, row) in enumerate(zip(pair, rows)):
            pbuf[row] = total[place]
            send(
                pbuf.at[row, :, twin], sibling_in.at[row], half_send, half_recv.at[by],
                device(me, twin),
            )
    for by in (2, 1, 3, 0):
        row = shifted("x", by)["x"]
        take(sibling_in.at[row], half_recv.at[by])
        pbuf[row, :, core] = pbuf[row, :, core] + sibling_in[row]
        share_out[row] = pbuf[row, :, core].astype(jnp.bfloat16)
        for dy in (4, 3, 5, 2, 6, 1, 7, 0):
            if by or dy:
                to = moved({"x": by, "y": dy, "z": 0})
                send(
                    share_out.at[to["x"], to["y"]], share_in.at[by * NY + dy - 1],
                    share_send, share_recv, device(to),
                )
    take(share_in, share_recv)
    result = pbuf[x, y, core] + jnp.sum(share_in[...].astype(jnp.float32), axis=0)
    out_ref[0] = (result * (NX * NY * NC * slots) ** -0.5).astype(out_ref.dtype)

    for unit, last in enumerate(LAST):
        take(share_in.at[:, :, pl.ds(0, COLS)], plane_send.at[unit])
        take(part(unit, everything), ring_send.at[unit])
        take(part(unit, {**everything, last: pl.ds(0, SIZES[last] - 1)}), twin_send.at[unit])
    take(sibling_in, half_send)
    take(share_in, share_send)


def shards(wavefunction, left_ops, right_ops, in_sector, counts):
    slots, rows, depth = left_ops.shape
    held = wavefunction.shape[1]
    columns = wavefunction.shape[2]
    dma = pltpu.SemaphoreType.DMA
    return pl.pallas_call(
        kernel,
        out_shape=jax.ShapeDtypeStruct(wavefunction.shape, wavefunction.dtype),
        in_specs=[
            pl.BlockSpec(memory_space=pltpu.VMEM),
            pl.BlockSpec(memory_space=pl.ANY),
            pl.BlockSpec(memory_space=pl.ANY),
            pl.BlockSpec(memory_space=pltpu.SMEM),
            pl.BlockSpec(memory_space=pltpu.SMEM),
        ],
        out_specs=pl.BlockSpec(memory_space=pltpu.VMEM),
        scratch_shapes=[
            pltpu.VMEM((UNITS, NZ, NX, NY, NC, held, COLS), jnp.bfloat16),
            pltpu.VMEM((slots, rows, depth), jnp.bfloat16),
            pltpu.VMEM((slots, columns, columns), jnp.bfloat16),
            pltpu.VMEM((slots, rows, columns), jnp.bfloat16),
            pltpu.VMEM((NX, NY, NC, held, columns), jnp.float32),
            pltpu.VMEM((NX, NY, held, columns), jnp.float32),
            pltpu.VMEM((NX, NY, held, columns), jnp.bfloat16),
            pltpu.VMEM((PEERS, held, columns), jnp.bfloat16),
            dma((2, slots)),
            dma((UNITS,)),
            dma((UNITS,)),
            dma((UNITS,)),
            dma((UNITS,)),
            dma((UNITS, NX * NY // 2, 2)),
            dma((UNITS,)),
            dma((UNITS,)),
            dma((UNITS,)),
            dma,
            dma((NX,)),
            dma,
            dma,
        ],
        compiler_params=pltpu.CompilerParams(collective_id=0, has_side_effects=True),
    )(wavefunction, left_ops, right_ops, in_sector, counts.T)


def solution(mesh):
    placed = (
        P("sec", "op", None),
        P(("op", "sec"), None, None),
        P(("op", "sec"), None, None),
        P(("op", "sec")),
        P(),
    )
    return jax.shard_map(
        shards, mesh=mesh, in_specs=placed, out_specs=P("sec", "op", None), check_vma=False
    )
```
